32 devices in a mesh: grp: 2 (over x), ctx: 16 (over z, y, core).
Axes of the slice: x: 2, y: 2, z: 4, core: 2. Of those that a mesh axis runs over, the one named last changes fastest.
Arguments:
- queries: bfloat16 [4, 12, 64, 128], P(None, 'grp'), parts along dimension 1, may hold values from -150 to 150
- key_cache: bfloat16 [12, 8, 2048, 128], P('grp', None, 'ctx'), parts along dimension 0, may hold values from -6 to 6
- value_cache: bfloat16 [12, 8, 2048, 128], P('grp', None, 'ctx'), parts along dimension 0, may hold values from -6 to 6
- row_lengths: int32 [12], P('grp'), parts along dimension 0, may hold values from 128 to 2048, as said below
- kept_tiles: int32 [4, 12, 16], P(None, 'grp'), parts along dimension 1, may hold values from 0 to 1, as said below
- tile_dest: int32 [12, 8, 16], P('grp'), parts along dimension 0, may hold values from 0 to 15, as said below
Outputs:
- attn_out: bfloat16 [4, 12, 64, 128], P(None, 'grp'), parts along dimension 1
- tile_mass: float32 [12, 8, 16], P('grp', None, 'ctx'), parts along dimension 0
- moved_keys: bfloat16 [12, 8, 2048, 128], P('grp', None, 'ctx'), parts along dimension 0
- moved_values: bfloat16 [12, 8, 2048, 128], P('grp', None, 'ctx'), parts along dimension 0
The draws below stay inside these ranges and needn't reach their ends.
There are 2 independent parts, one for each index of `grp`. The reference program is written for one: setup_inputs(seed, part) draws one part's arguments, and reference() takes and returns one part's arrays. A program takes and returns all parts, laid end to end along the dimension named above; each array names one. Nothing has to cross between parts.
Inputs may be any that keep to these rules, and one draw needn't show every extreme that they name: `row_lengths`: at least 128 positions of every row are filled; some row is filled to all 2048 positions. `kept_tiles`: A tile dropped at one step stays dropped at all later steps; tile 0 of every row is kept at every step. For each row and head, tile_dest is a permutation of the 16 tiles. The 1 tiles that one index of ctx holds for a row and head all go, in some order, to the index a per-row-and-head offset further along ctx, wrapping around; that offset is the same for every index. No offset is used by more than 3 row-head pairs, and some offset is used by exactly 3. The offsets 16 // 2 and 1 are used by some row-head pair in every draw.
All inputs are finite; a program needn't handle non-finite values.
Results may differ from the reference program's by a relative error of at most 0.0027.
Values may be sent and summed in bfloat16 or wider, within the bound.
A program may use at most 64 MiB of HBM per device.

```python
import jax
import jax.numpy as jnp
from jax import lax

QH = 64
KVH = 8
HD = 128
TILE = 128
STEPS = 4
ROWS = 6
TILES_DEV = 1
TILES = 16
SLOTS = 2048
N_CTX = 16


def draw_key_cache(key, part):
    drawn = jnp.clip(jax.random.normal(jax.random.fold_in(key, 32), (ROWS, KVH, SLOTS, HD), jnp.float32), -6.0, 6.0)
    return drawn.astype(jnp.bfloat16)


def draw_queries(key, part):
    drawn = 3.0 * jnp.clip(jax.random.normal(jax.random.fold_in(key, 33), (STEPS, ROWS, QH, HD), jnp.float32), -6.0, 6.0)
    return drawn.astype(jnp.bfloat16)


def draw_row_lengths(key, part):
    drawn = jax.random.randint(jax.random.fold_in(key, 41), (ROWS,), TILE, SLOTS + 1)
    longest = jax.random.randint(jax.random.fold_in(key, 42), (), 0, ROWS)
    return drawn.at[longest].set(SLOTS).astype(jnp.int32)


def draw_kept_tiles(key, part):
    evict_step = jax.random.randint(jax.random.fold_in(key, 51), (ROWS, TILES), 0, 2 * STEPS)
    evict_step = evict_step.at[:, 0].set(2 * STEPS)
    steps_index = jnp.arange(STEPS, dtype=jnp.int32)[:, None, None]
    return (steps_index < evict_step[None, :, :]).astype(jnp.int32)


def swap_front(values, wanted, place):
    where_found = jnp.argmax((values == wanted).astype(jnp.int32))
    current = values[place]
    return values.at[where_found].set(current).at[place].set(wanted)


def draw_tile_dest(key, part):
    pair_count = ROWS * KVH
    pair_order = jax.random.permutation(jax.random.fold_in(key, 61), pair_count)
    shift_pick = jax.random.permutation(jax.random.fold_in(key, 62), N_CTX).astype(jnp.int32)
    shift_pick = swap_front(shift_pick, N_CTX // 2, 0)
    shift_pick = swap_front(shift_pick, 1, 1)
    offsets = shift_pick[pair_order % N_CTX].reshape(ROWS, KVH)
    slot_scores = jax.random.randint(jax.random.fold_in(key, 63), (ROWS, KVH, N_CTX, TILES_DEV), 0, 1 << 20)
    slot_scores = slot_scores * TILES_DEV + jnp.arange(TILES_DEV, dtype=jnp.int32)
    slot_order = jnp.argsort(slot_scores, axis=-1, stable=True)
    devices = jnp.arange(N_CTX, dtype=jnp.int32)[None, None, :, None]
    target = (devices + offsets[:, :, None, None]) % N_CTX * TILES_DEV + slot_order
    return target.reshape(ROWS, KVH, TILES).astype(jnp.int32)


def shard_levels(rng, dims, shards, smallest, largest):
    loudness = 1.0
    for dim, shards_of in shards:
        draws = jax.random.uniform(jax.random.fold_in(jax.random.fold_in(rng, 6), dim), (shards_of,), jnp.float32, smallest / len(shards), largest / len(shards))
        loudness = loudness * jnp.repeat(jnp.exp(draws), dims[dim] // shards_of).reshape((-1,) + (1,) * (len(dims) - 1 - dim))
    return loudness


def normal_values(key, dims, width, reach, cuts=(), kind=jnp.bfloat16):
    loudness = shard_levels(key, dims, cuts, -0.22, 0.18) if cuts else 1.0
    result = jax.random.normal(key, dims, jnp.float32) * width * loudness
    return jnp.minimum(jnp.maximum(result, -reach), reach).astype(kind)


def setup_inputs(seed: int = 0, part: int = 0) -> dict:
    splits = jax.random.split(jax.random.key(seed), 7)
    own_keys = jax.random.split(jax.random.fold_in(splits[6], part), 7)
    return {
        "queries": draw_queries(jax.random.fold_in(jax.random.fold_in(splits[6], part), 71), part),
        "key_cache": draw_key_cache(jax.random.fold_in(jax.random.fold_in(splits[6], part), 71), part),
        "value_cache": normal_values(own_keys[2], (ROWS, KVH, SLOTS, HD), 1.0, 6.0, ((2, 16),)),
        "row_lengths": draw_row_lengths(jax.random.fold_in(jax.random.fold_in(splits[6], part), 71), part),
        "kept_tiles": draw_kept_tiles(jax.random.fold_in(jax.random.fold_in(splits[6], part), 71), part),
        "tile_dest": draw_tile_dest(jax.random.fold_in(jax.random.fold_in(splits[6], part), 71), part),
    }


absent_score = -1e30


def row_attention(inputs):
    query_row, key_row, value_row, length, kept_row = inputs
    group_size = QH // KVH
    block_len = TILES_DEV * TILE
    grouped = query_row.astype(jnp.float32).reshape(STEPS, KVH, group_size, HD)
    key_blocks = key_row.astype(jnp.float32).reshape(KVH, N_CTX, block_len, HD)
    value_blocks = value_row.astype(jnp.float32).reshape(KVH, N_CTX, block_len, HD)
    scores = jnp.einsum("shgd,hnbd->shgnb", grouped, key_blocks) * (HD ** -0.5)
    positions = jnp.arange(SLOTS, dtype=jnp.int32)
    live_mask = (jnp.repeat(kept_row, TILE, axis=1) > 0) & (positions[None, :] < length)
    live_mask = live_mask.reshape(STEPS, 1, 1, N_CTX, block_len)
    block_peak = jnp.max(jnp.where(live_mask, scores, absent_score), axis=-1)
    weights = jnp.where(live_mask, jnp.exp(scores - block_peak[..., None]), 0.0)
    block_total = jnp.sum(weights, axis=-1)
    rounded = lax.optimization_barrier(weights.astype(jnp.bfloat16)).astype(jnp.float32)
    block_out = jnp.einsum("shgnb,hnbd->shgnd", rounded, value_blocks)
    score_peak = jnp.max(block_peak, axis=-1)
    factor = jnp.exp(block_peak - score_peak[..., None])
    denominator = jnp.sum(block_total * factor, axis=-1)
    summed = jnp.sum(block_out * factor[..., None], axis=3)
    attended = (summed / denominator[..., None]).astype(jnp.bfloat16).reshape(STEPS, QH, HD)
    coefficient = factor / denominator[..., None]
    tile_sums = jnp.einsum("shgnb,shgn->hnb", weights, coefficient, precision=lax.Precision.HIGHEST)
    tile_sums = tile_sums.reshape(KVH, N_CTX, TILES_DEV, TILE).sum(-1).reshape(KVH, TILES)
    return attended, tile_sums


def relocate(cache, tile_dest):
    tile_blocks = cache.reshape(ROWS, KVH, TILES, TILE, HD)
    row_index = jnp.arange(ROWS, dtype=jnp.int32)[:, None, None]
    head_index = jnp.arange(KVH, dtype=jnp.int32)[None, :, None]
    placed = jnp.zeros_like(tile_blocks).at[row_index, head_index, tile_dest].set(tile_blocks)
    return placed.reshape(cache.shape)


def reference(queries, key_cache, value_cache, row_lengths, kept_tiles, tile_dest):
    attended, tile_mass = lax.map(
        row_attention,
        (jnp.moveaxis(queries, 1, 0), key_cache, value_cache, row_lengths, jnp.moveaxis(kept_tiles, 1, 0)),
    )
    attn_out = jnp.moveaxis(attended, 0, 1)
    return attn_out, tile_mass, relocate(key_cache, tile_dest), relocate(value_cache, tile_dest)
```

```python
import functools

import jax
import jax.numpy as jnp
from jax import lax
from jax.experimental import pallas as pl
from jax.experimental.pallas import tpu as pltpu
from jax.sharding import PartitionSpec as P

QH = 64
KVH = 8
HD = 128
TILE = 128
STEPS = 4
LANES = 128
STAT_ROWS = 8

absent_score = -1e30


def fold_stats(peaks, totals):
    top = functools.reduce(jnp.maximum, peaks)
    factors = [jnp.exp(peak - top) for peak in peaks]
    total = sum(factor * part for factor, part in zip(factors, totals))
    return top, total, factors


def columns_of(rows):
    height = len(rows)
    filler = jnp.zeros((LANES - height, LANES), jnp.float32)
    return jnp.transpose(jnp.concatenate(list(rows) + [filler], axis=0))


def stat_block(top, total):
    return jnp.concatenate([top, total, jnp.zeros((STAT_ROWS - 2, LANES), jnp.float32)], axis=0)


def main_kernel(
    device_count, plane, group_count,
    order_ref, lengths_ref, kept_ref, queries_hbm, keys_hbm, values_hbm,
    arrived_ref, attn_ref, mass_ref,
    queries_ref, keys_ref, values_ref, load_sem, staged, parts, columns, stats, parts_in, stats_in, merged, merged_stats,
    merged_in, merged_stats_in, final, final_stats,
    own_sem, move_send, move_recv, a_send, a_recv, b_send, b_recv, c_send, c_recv, d_send, d_recv,
):
    me = lax.axis_index("ctx")
    outer = device_count // plane
    row_count, head_count = keys_ref.shape[:2]
    pair_count = row_count * head_count
    steps = queries_ref.shape[0]
    group_size = queries_ref.shape[2] // head_count
    pair_rows = steps * group_size
    owner_rows = group_count * pair_rows
    my_outer = me // plane
    my_column = me % plane

    barrier = pltpu.get_barrier_semaphore()
    for step in range(1, device_count):
        pl.semaphore_signal(barrier, inc=1, device_id={"ctx": (me + step) % device_count})

    loads = [
        pltpu.make_async_copy(src, dst, load_sem.at[which])
        for which, (src, dst) in enumerate(
            ((keys_hbm, keys_ref), (values_hbm, values_ref), (queries_hbm, queries_ref))
        )
    ]
    for load in loads:
        load.start()
    for load in loads:
        load.wait()

    @pl.loop(0, device_count * group_count)
    def _(slot):
        pair = order_ref[slot]
        row, head = pair // head_count, pair % head_count
        staged[slot, 0] = keys_ref[row, head]
        staged[slot, 1] = values_ref[row, head]

    pl.semaphore_wait(barrier, device_count - 1)

    own = pltpu.make_async_copy(
        staged.at[pl.ds(0, group_count)], arrived_ref.at[pl.ds(0, group_count)], own_sem
    )
    own.start()

    lower = my_outer < outer // 2
    near_count = outer // 2 if outer % 2 == 0 else outer
    mirrored = jnp.where(lower, my_outer, outer - 1 - my_outer)

    def move(level_kind, level_index, half_flip, side_flip):
        if level_kind == "far":
            level = outer - 1 - level_index
        else:
            level = (mirrored + level_index) % near_count
        level = jnp.where(lower, level, outer - 1 - level)
        half, side = my_column // sides, my_column % sides
        column = (half + half_flip) % halves * sides + (side + side_flip) % sides
        target = level * plane + column
        offset = (target - me + device_count) % device_count
        window = pl.ds(offset * group_count, group_count)
        return pltpu.make_async_remote_copy(
            src_ref=staged.at[window],
            dst_ref=arrived_ref.at[window],
            send_sem=move_send.at[offset],
            recv_sem=move_recv.at[offset],
            device_id={"ctx": target},
        )

    halves = 2 if plane % 2 == 0 else 1
    sides = plane // halves
    far = [("far", k) for k in range(outer - near_count)]
    near = [("near", k) for k in range(1, near_count)]
    own_level = [("near", 0)]
    first_far, second_far = far[: len(far) // 2], far[len(far) // 2 :]

    def to_columns(levels, half_flip):
        if half_flip >= halves:
            return []
        return [(*level, half_flip, side) for side in range(sides) for level in levels]

    batches = [
        to_columns(first_far, 0) + to_columns(near, 0) + to_columns(own_level, 0)[1:],
        to_columns(second_far, 0) + to_columns(near, 1)[: len(near)],
        to_columns(first_far, 1) + to_columns(second_far, 1) + to_columns(near, 1)[len(near) :] + to_columns(own_level, 1),
    ]
    turns = [turn for batch in batches for turn in batch]
    assert len(turns) == device_count - 1

    def start_moves(batch):
        for turn in batches[batch]:
            move(*turn).start()

    start_moves(0)

    lane = lax.broadcasted_iota(jnp.int32, (pair_rows, TILE), 1)
    step_of = lax.broadcasted_iota(jnp.int32, (pair_rows, TILE), 0) // group_size
    if device_count * group_count > pair_count:
        parts[...] = jnp.zeros_like(parts)
    columns[...] = jnp.zeros_like(columns)

    @pl.loop(0, row_count)
    def _(row):
        filled = lengths_ref[row] - me * TILE
        limit = jnp.zeros((pair_rows, TILE), jnp.int32)
        for step in range(steps):
            here = jnp.where(kept_ref[row, step, me] > 0, filled, 0)
            limit = jnp.where(step_of == step, here, limit)
        live = lane < limit
        query_rows = [queries_ref[step, row].astype(jnp.float32) for step in range(steps)]
        scores = []
        for head in range(head_count):
            span = slice(head * group_size, (head + 1) * group_size)
            query = jnp.concatenate([q[span] for q in query_rows], axis=0).astype(jnp.bfloat16)
            scores.append(lax.dot_general(
                query, keys_ref[row, head], (((1,), (1,)), ((), ())),
                preferred_element_type=jnp.float32,
            ))
        scores = jnp.stack(scores) * HD ** (-0.5)
        peak = jnp.max(jnp.where(live[None], scores, absent_score), axis=2, keepdims=True)
        weights = jnp.where(live[None], jnp.exp(scores - peak), 0.0)
        total = jnp.sum(weights, axis=2, keepdims=True)
        both = jnp.where(lane[None] == 0, peak, total)
        rounded = weights.astype(jnp.bfloat16)
        for head in range(head_count):
            pair = row * head_count + head
            owner, slot = pair // group_count, pair % group_count
            place = pl.ds(pl.multiple_of(slot * pair_rows, pair_rows), pair_rows)
            parts[owner % plane, owner // plane, place] = jnp.dot(
                rounded[head], values_ref[row, head], preferred_element_type=jnp.float32
            )
            columns[owner, place] = both[head]

    @pl.loop(0, device_count)
    def _(owner):
        turned = jnp.transpose(columns[owner])
        stats[owner % plane, owner // plane] = turned[:STAT_ROWS]

    sends_a = []
    for step in range(1, plane):
        peer = (my_column + step) % plane
        target = my_outer * plane + peer
        for which, (src, dst) in enumerate(((parts, parts_in), (stats, stats_in))):
            sends_a.append(pltpu.make_async_remote_copy(
                src_ref=src.at[peer], dst_ref=dst.at[step - 1],
                send_sem=a_send.at[which, step - 1], recv_sem=a_recv.at[which, step - 1],
                device_id={"ctx": target},
            ))
    for copy in sends_a:
        copy.start()
    for copy in sends_a:
        copy.wait_recv()

    @pl.loop(0, outer)
    def _(level):
        blocks = [stats[my_column, level]] + [stats_in[k, level] for k in range(plane - 1)]
        top, total, factors = fold_stats([b[0:1] for b in blocks], [b[1:2] for b in blocks])
        scale = columns_of(factors)[:owner_rows]
        summed = scale[:, 0:1] * parts[my_column, level]
        for k in range(plane - 1):
            summed += scale[:, k + 1 : k + 2] * parts_in[k, level]
        merged[level] = summed
        merged_stats[level] = stat_block(top, total)

    sends_b = []
    for step in range(1, outer):
        level = (my_outer + step) % outer
        for which, (src, dst) in enumerate(((merged, merged_in), (merged_stats, merged_stats_in))):
            sends_b.append(pltpu.make_async_remote_copy(
                src_ref=src.at[level], dst_ref=dst.at[step - 1],
                send_sem=b_send.at[which, step - 1], recv_sem=b_recv.at[which, step - 1],
                device_id={"ctx": level * plane + my_column},
            ))
    for copy in sends_b:
        copy.start()
    start_moves(1)
    for copy in sends_b:
        copy.wait_recv()

    blocks = [merged_stats[my_outer]] + [merged_stats_in[k] for k in range(outer - 1)]
    top, total, factors = fold_stats([b[0:1] for b in blocks], [b[1:2] for b in blocks])
    scale = columns_of(factors + [total])[:owner_rows]
    summed = scale[:, 0:1] * merged[my_outer]
    for k in range(outer - 1):
        summed += scale[:, k + 1 : k + 2] * merged_in[k]
    final[my_column, my_outer] = (summed / scale[:, outer : outer + 1]).astype(jnp.bfloat16)
    final_stats[my_column, my_outer] = stat_block(top, total)

    sends_c = []
    for step in range(1, outer):
        level = (my_outer + step) % outer
        for which, ref in enumerate((final, final_stats)):
            sends_c.append(pltpu.make_async_remote_copy(
                src_ref=ref.at[my_column, my_outer], dst_ref=ref.at[my_column, my_outer],
                send_sem=c_send.at[which, step - 1], recv_sem=c_recv.at[which, step - 1],
                device_id={"ctx": level * plane + my_column},
            ))
    for copy in sends_c:
        copy.start()
    start_moves(2)
    for copy in sends_c:
        copy.wait_recv()
    sends_d = []
    for step in range(1, plane):
        target = my_outer * plane + (my_column + step) % plane
        for which, ref in enumerate((final, final_stats)):
            sends_d.append(pltpu.make_async_remote_copy(
                src_ref=ref.at[my_column], dst_ref=ref.at[my_column],
                send_sem=d_send.at[which, step - 1], recv_sem=d_recv.at[which, step - 1],
                device_id={"ctx": target},
            ))
    for copy in sends_d:
        copy.start()
    for copy in sends_d:
        copy.wait_recv()

    for row in range(row_count):
        pieces = []
        for head in range(head_count):
            owner, slot = divmod(row * head_count + head, group_count)
            span = slice(slot * pair_rows, (slot + 1) * pair_rows)
            pieces.append(final[owner % plane, owner // plane, span].astype(jnp.float32))
        for step in range(steps):
            span = slice(step * group_size, (step + 1) * group_size)
            attn_ref[step, row] = jnp.concatenate([p[span] for p in pieces], axis=0).astype(jnp.bfloat16)

    group_of = lax.broadcasted_iota(jnp.int32, (1, LANES), 1) // pair_rows
    masses = []
    for pair in range(pair_count):
        owner, slot = divmod(pair, group_count)
        own_stats = stats[owner % plane, owner // plane]
        all_stats = final_stats[owner % plane, owner // plane]
        factor = jnp.exp(own_stats[0:1] - all_stats[0:1])
        mass = own_stats[1:2] * factor / all_stats[1:2]
        masses.append(jnp.where(group_of == slot, mass, 0.0))
    mass_row = jnp.sum(columns_of(masses), axis=0, keepdims=True)
    for row in range(row_count):
        mass_ref[row] = mass_row[:, row * head_count : (row + 1) * head_count]

    own.wait()
    for copy in sends_a + sends_b + sends_c + sends_d:
        copy.wait_send()
    for turn in turns:
        move(*turn).wait_send()
    for turn in turns:
        move(*turn).wait_recv()


def place_kernel(
    slot_ref, arrived_hbm, attn_ref, mass_ref, keys_out, values_out, attn_out, mass_out,
    arrived_ref, keys_ref, values_ref, attn_held, in_sem, out_sem,
):
    row_count, head_count = keys_out.shape[:2]
    loads = [
        pltpu.make_async_copy(arrived_hbm.at[:, which], arrived_ref.at[which], in_sem.at[which])
        for which in range(2)
    ]
    for load in loads:
        load.start()
    small = pltpu.make_async_copy(attn_ref, attn_held, in_sem.at[2])
    small.start()
    mass_out[...] = mass_ref[...]
    small.wait()
    out = [pltpu.make_async_copy(attn_held, attn_out, out_sem.at[2, 0])]
    out[0].start()
    for which, (held, placed) in enumerate(((keys_ref, keys_out), (values_ref, values_out))):
        loads[which].wait()
        for row in range(row_count):
            for head in range(head_count):
                held[row, head] = arrived_ref[which, slot_ref[row * head_count + head]]
            out.append(pltpu.make_async_copy(held.at[row], placed.at[row], out_sem.at[which, row]))
            out[-1].start()
    for copy in out:
        copy.wait()


def local(queries, key_cache, value_cache, row_lengths, kept_tiles, tile_dest):
    device_count = lax.axis_size("ctx")
    plane = 4 if device_count % 4 == 0 and device_count > 4 else 1
    outer = device_count // plane
    row_count, head_count, token_span, width = key_cache.shape
    pair_count = row_count * head_count
    group_count = -(-pair_count // device_count)
    pair_rows = STEPS * (QH // head_count)
    owner_rows = group_count * pair_rows
    slots = device_count * group_count
    assert owner_rows <= LANES and token_span == TILE

    offsets = (tile_dest[:, :, 0] % device_count).reshape(pair_count)
    index = jnp.arange(pair_count, dtype=jnp.int32)
    earlier = (index[:, None] > index[None, :]) & (offsets[:, None] == offsets[None, :])
    slot_of = offsets * group_count + jnp.sum(earlier.astype(jnp.int32), axis=1)
    hit = slot_of[:, None] == jnp.arange(slots, dtype=jnp.int32)[None, :]
    order = jnp.sum(jnp.where(hit, index[:, None], 0), axis=0)

    smem = pl.BlockSpec(memory_space=pltpu.SMEM)
    vmem = pl.BlockSpec(memory_space=pltpu.VMEM)
    hbm = pl.BlockSpec(memory_space=pltpu.HBM)
    sems = pltpu.SemaphoreType.DMA
    arrived, attn_out, mass = pl.pallas_call(
        functools.partial(main_kernel, device_count, plane, group_count),
        out_shape=(
            jax.ShapeDtypeStruct((slots, 2, TILE, width), jnp.bfloat16),
            jax.ShapeDtypeStruct(queries.shape, jnp.bfloat16),
            jax.ShapeDtypeStruct((row_count, 1, head_count), jnp.float32),
        ),
        in_specs=[smem, smem, smem, hbm, hbm, hbm],
        out_specs=(hbm, vmem, vmem),
        scratch_shapes=[
            pltpu.VMEM(queries.shape, jnp.bfloat16),
            pltpu.VMEM(key_cache.shape, jnp.bfloat16),
            pltpu.VMEM(value_cache.shape, jnp.bfloat16),
            sems((3,)),
            pltpu.VMEM((slots, 2, TILE, width), jnp.bfloat16),
            pltpu.VMEM((plane, outer, owner_rows, width), jnp.float32),
            pltpu.VMEM((device_count, LANES, LANES), jnp.float32),
            pltpu.VMEM((plane, outer, STAT_ROWS, LANES), jnp.float32),
            pltpu.VMEM((plane - 1, outer, owner_rows, width), jnp.float32),
            pltpu.VMEM((plane - 1, outer, STAT_ROWS, LANES), jnp.float32),
            pltpu.VMEM((outer, owner_rows, width), jnp.float32),
            pltpu.VMEM((outer, STAT_ROWS, LANES), jnp.float32),
            pltpu.VMEM((outer - 1, owner_rows, width), jnp.float32),
            pltpu.VMEM((outer - 1, STAT_ROWS, LANES), jnp.float32),
            pltpu.VMEM((plane, outer, owner_rows, width), jnp.bfloat16),
            pltpu.VMEM((plane, outer, STAT_ROWS, LANES), jnp.float32),
            sems,
            sems((device_count,)),
            sems((device_count,)),
            sems((2, plane - 1)),
            sems((2, plane - 1)),
            sems((2, outer - 1)),
            sems((2, outer - 1)),
            sems((2, outer - 1)),
            sems((2, outer - 1)),
            sems((2, plane - 1)),
            sems((2, plane - 1)),
        ],
        compiler_params=pltpu.CompilerParams(
            collective_id=0, has_side_effects=True, vmem_limit_bytes=63 * 1024 * 1024
        ),
        name="attend_and_move",
    )(order, row_lengths, jnp.swapaxes(kept_tiles, 0, 1), queries, key_cache, value_cache)

    moved_keys, moved_values, attn_out, tile_mass = pl.pallas_call(
        place_kernel,
        out_shape=(
            jax.ShapeDtypeStruct(key_cache.shape, jnp.bfloat16),
            jax.ShapeDtypeStruct(value_cache.shape, jnp.bfloat16),
            jax.ShapeDtypeStruct(attn_out.shape, attn_out.dtype),
            jax.ShapeDtypeStruct(mass.shape, mass.dtype),
        ),
        in_specs=[smem, hbm, hbm, vmem],
        out_specs=(hbm, hbm, hbm, vmem),
        scratch_shapes=[
            pltpu.VMEM((2, slots, TILE, width), jnp.bfloat16),
            pltpu.VMEM(key_cache.shape, jnp.bfloat16),
            pltpu.VMEM(value_cache.shape, jnp.bfloat16),
            pltpu.VMEM(attn_out.shape, attn_out.dtype),
            sems((3,)),
            sems((3, row_count)),
        ],
        compiler_params=pltpu.CompilerParams(vmem_limit_bytes=63 * 1024 * 1024),
        name="place",
    )(slot_of, arrived, attn_out, mass)
    return attn_out, jnp.swapaxes(tile_mass, 1, 2), moved_keys, moved_values


def solution(mesh):
    in_specs = (
        P(None, "grp", None, None),
        P("grp", None, "ctx", None),
        P("grp", None, "ctx", None),
        P("grp"),
        P(None, "grp", None),
        P("grp", None, None),
    )
    out_specs = (
        P(None, "grp", None, None),
        P("grp", None, "ctx"),
        P("grp", None, "ctx", None),
        P("grp", None, "ctx", None),
    )
    return jax.shard_map(local, mesh=mesh, in_specs=in_specs, out_specs=out_specs, check_vma=False)
```

```python
import functools

import jax
import jax.numpy as jnp
from jax import lax
from jax.experimental import pallas as pl
from jax.experimental.pallas import tpu as pltpu
from jax.sharding import PartitionSpec as P

QH = 64
KVH = 8
HD = 128
TILE = 128
STEPS = 4
LANES = 128
STAT_ROWS = 8

absent_score = -1e30


def fold_stats(peaks, totals):
    top = functools.reduce(jnp.maximum, peaks)
    factors = [jnp.exp(peak - top) for peak in peaks]
    total = sum(factor * part for factor, part in zip(factors, totals))
    return top, total, factors


def columns_of(rows):
    height = len(rows)
    filler = jnp.zeros((LANES - height, LANES), jnp.float32)
    return jnp.transpose(jnp.concatenate(list(rows) + [filler], axis=0))


def stat_block(top, total):
    return jnp.concatenate([top, total, jnp.zeros((STAT_ROWS - 2, LANES), jnp.float32)], axis=0)


def slots_of(dest, group_count):
    row_count, head_count, tiles = dest.shape
    pair_count = row_count * head_count
    offset = jnp.broadcast_to(dest.reshape(pair_count, tiles)[:, 0:1], (pair_count, LANES))
    filler = jnp.full((LANES - pair_count, LANES), -1, jnp.int32)
    across = jnp.transpose(jnp.concatenate([offset, filler], axis=0))[:pair_count]
    pair = lax.broadcasted_iota(jnp.int32, (pair_count, LANES), 0)
    lane = lax.broadcasted_iota(jnp.int32, (pair_count, LANES), 1)
    earlier = jnp.where((offset == across) & (lane < pair), 1, 0)
    slot = offset[:, 0:1] * group_count + jnp.sum(earlier, axis=1, keepdims=True)
    order = jnp.sum(jnp.where(slot == lane, pair, 0), axis=0, keepdims=True)
    spread = jnp.concatenate([jnp.broadcast_to(slot, (pair_count, LANES)), filler], axis=0)
    return order, jnp.transpose(spread)[0:1]


def main_kernel(
    device_count, plane, group_count,
    lengths_hbm, kept_hbm, dest_hbm, queries_hbm, keys_hbm, values_hbm,
    arrived_ref, attn_ref, mass_ref, slot_ref,
    lengths_ref, kept_ref, dest_ref, order_row, order_ref, order_sem, queries_ref, keys_ref, values_ref, load_sem, staged, parts, columns, stats, parts_in, stats_in, merged, merged_stats,
    merged_in, merged_stats_in, final, final_stats,
    own_sem, move_send, move_recv, a_send, a_recv, b_send, b_recv, c_send, c_recv, d_send, d_recv,
):
    me = lax.axis_index("ctx")
    outer = device_count // plane
    row_count, head_count = keys_ref.shape[:2]
    pair_count = row_count * head_count
    steps = queries_ref.shape[0]
    group_size = queries_ref.shape[2] // head_count
    pair_rows = steps * group_size
    owner_rows = group_count * pair_rows
    my_outer = me // plane
    my_column = me % plane

    barrier = pltpu.get_barrier_semaphore()
    for step in range(1, device_count):
        pl.semaphore_signal(barrier, inc=1, device_id={"ctx": (me + step) % device_count})

    dest_load = pltpu.make_async_copy(dest_hbm, dest_ref, order_sem.at[0])
    dest_load.start()
    loads = [
        pltpu.make_async_copy(src, dst, load_sem.at[which])
        for which, (src, dst) in enumerate(
            (
                (keys_hbm, keys_ref), (values_hbm, values_ref), (queries_hbm, queries_ref),
                (lengths_hbm, lengths_ref), (kept_hbm, kept_ref),
            )
        )
    ]
    for load in loads:
        load.start()

    dest_load.wait()
    order_row[...], slot_ref[...] = slots_of(dest_ref[...], group_count)
    order_copy = pltpu.make_async_copy(order_row, order_ref, order_sem.at[1])
    order_copy.start()
    for load in loads:
        load.wait()
    order_copy.wait()

    @pl.loop(0, device_count * group_count)
    def _(slot):
        pair = order_ref[0, slot]
        row, head = pair // head_count, pair % head_count
        staged[slot, 0] = keys_ref[row, head]
        staged[slot, 1] = values_ref[row, head]

    pl.semaphore_wait(barrier, device_count - 1)

    own = pltpu.make_async_copy(
        staged.at[pl.ds(0, group_count)], arrived_ref.at[pl.ds(0, group_count)], own_sem
    )
    own.start()

    lower = my_outer < outer // 2
    near_count = outer // 2 if outer % 2 == 0 else outer
    mirrored = jnp.where(lower, my_outer, outer - 1 - my_outer)

    def move(level_kind, level_index, half_flip, side_flip):
        if level_kind == "far":
            level = outer - 1 - level_index
        else:
            level = (mirrored + level_index) % near_count
        level = jnp.where(lower, level, outer - 1 - level)
        half, side = my_column // sides, my_column % sides
        column = (half + half_flip) % halves * sides + (side + side_flip) % sides
        target = level * plane + column
        offset = (target - me + device_count) % device_count
        window = pl.ds(offset * group_count, group_count)
        return pltpu.make_async_remote_copy(
            src_ref=staged.at[window],
            dst_ref=arrived_ref.at[window],
            send_sem=move_send.at[offset],
            recv_sem=move_recv.at[offset],
            device_id={"ctx": target},
        )

    halves = 2 if plane % 2 == 0 else 1
    sides = plane // halves
    far = [("far", k) for k in range(outer - near_count)]
    near = [("near", k) for k in range(1, near_count)]
    own_level = [("near", 0)]
    first_far, second_far = far[: len(far) // 2], far[len(far) // 2 :]

    def to_columns(levels, half_flip):
        if half_flip >= halves:
            return []
        return [(*level, half_flip, side) for side in range(sides) for level in levels]

    batches = [
        to_columns(first_far, 0) + to_columns(near, 0) + to_columns(own_level, 0)[1:],
        to_columns(second_far, 0) + to_columns(near, 1)[: len(near)],
        to_columns(first_far, 1) + to_columns(second_far, 1) + to_columns(near, 1)[len(near) :] + to_columns(own_level, 1),
    ]
    turns = [turn for batch in batches for turn in batch]
    assert len(turns) == device_count - 1

    def start_moves(batch):
        for turn in batches[batch]:
            move(*turn).start()

    start_moves(0)

    lane = lax.broadcasted_iota(jnp.int32, (pair_rows, TILE), 1)
    step_of = lax.broadcasted_iota(jnp.int32, (pair_rows, TILE), 0) // group_size
    if device_count * group_count > pair_count:
        parts[...] = jnp.zeros_like(parts)
    columns[...] = jnp.zeros_like(columns)

    @pl.loop(0, row_count)
    def _(row):
        filled = lengths_ref[row] - me * TILE
        limit = jnp.zeros((pair_rows, TILE), jnp.int32)
        for step in range(steps):
            here = jnp.where(kept_ref[row, step, me] > 0, filled, 0)
            limit = jnp.where(step_of == step, here, limit)
        live = lane < limit
        query_rows = [queries_ref[step, row].astype(jnp.float32) for step in range(steps)]
        scores = []
        for head in range(head_count):
            span = slice(head * group_size, (head + 1) * group_size)
            query = jnp.concatenate([q[span] for q in query_rows], axis=0).astype(jnp.bfloat16)
            scores.append(lax.dot_general(
                query, keys_ref[row, head], (((1,), (1,)), ((), ())),
                preferred_element_type=jnp.float32,
            ))
        scores = jnp.stack(scores) * HD ** (-0.5)
        peak = jnp.max(jnp.where(live[None], scores, absent_score), axis=2, keepdims=True)
        weights = jnp.where(live[None], jnp.exp(scores - peak), 0.0)
        total = jnp.sum(weights, axis=2, keepdims=True)
        both = jnp.where(lane[None] == 0, peak, total)
        rounded = weights.astype(jnp.bfloat16)
        for head in range(head_count):
            pair = row * head_count + head
            owner, slot = pair // group_count, pair % group_count
            place = pl.ds(pl.multiple_of(slot * pair_rows, pair_rows), pair_rows)
            parts[owner % plane, owner // plane, place] = jnp.dot(
                rounded[head], values_ref[row, head], preferred_element_type=jnp.float32
            )
            columns[owner, place] = both[head]

    @pl.loop(0, device_count)
    def _(owner):
        turned = jnp.transpose(columns[owner])
        stats[owner % plane, owner // plane] = turned[:STAT_ROWS]

    sends_a = []
    for step in range(1, plane):
        peer = (my_column + step) % plane
        target = my_outer * plane + peer
        for which, (src, dst) in enumerate(((parts, parts_in), (stats, stats_in))):
            sends_a.append(pltpu.make_async_remote_copy(
                src_ref=src.at[peer], dst_ref=dst.at[step - 1],
                send_sem=a_send.at[which, step - 1], recv_sem=a_recv.at[which, step - 1],
                device_id={"ctx": target},
            ))
    for copy in sends_a:
        copy.start()
    for copy in sends_a:
        copy.wait_recv()

    @pl.loop(0, outer)
    def _(level):
        blocks = [stats[my_column, level]] + [stats_in[k, level] for k in range(plane - 1)]
        top, total, factors = fold_stats([b[0:1] for b in blocks], [b[1:2] for b in blocks])
        scale = columns_of(factors)[:owner_rows]
        summed = scale[:, 0:1] * parts[my_column, level]
        for k in range(plane - 1):
            summed += scale[:, k + 1 : k + 2] * parts_in[k, level]
        merged[level] = summed
        merged_stats[level] = stat_block(top, total)

    sends_b = []
    for step in range(1, outer):
        level = (my_outer + step) % outer
        for which, (src, dst) in enumerate(((merged, merged_in), (merged_stats, merged_stats_in))):
            sends_b.append(pltpu.make_async_remote_copy(
                src_ref=src.at[level], dst_ref=dst.at[step - 1],
                send_sem=b_send.at[which, step - 1], recv_sem=b_recv.at[which, step - 1],
                device_id={"ctx": level * plane + my_column},
            ))
    for copy in sends_b:
        copy.start()
    start_moves(1)
    for copy in sends_b:
        copy.wait_recv()

    blocks = [merged_stats[my_outer]] + [merged_stats_in[k] for k in range(outer - 1)]
    top, total, factors = fold_stats([b[0:1] for b in blocks], [b[1:2] for b in blocks])
    scale = columns_of(factors + [total])[:owner_rows]
    summed = scale[:, 0:1] * merged[my_outer]
    for k in range(outer - 1):
        summed += scale[:, k + 1 : k + 2] * merged_in[k]
    final[my_column, my_outer] = (summed / scale[:, outer : outer + 1]).astype(jnp.bfloat16)
    final_stats[my_column, my_outer] = stat_block(top, total)

    sends_c = []
    for step in range(1, outer):
        level = (my_outer + step) % outer
        for which, ref in enumerate((final, final_stats)):
            sends_c.append(pltpu.make_async_remote_copy(
                src_ref=ref.at[my_column, my_outer], dst_ref=ref.at[my_column, my_outer],
                send_sem=c_send.at[which, step - 1], recv_sem=c_recv.at[which, step - 1],
                device_id={"ctx": level * plane + my_column},
            ))
    for copy in sends_c:
        copy.start()
    start_moves(2)
    for copy in sends_c:
        copy.wait_recv()
    sends_d = []
    for step in range(1, plane):
        target = my_outer * plane + (my_column + step) % plane
        for which, ref in enumerate((final, final_stats)):
            sends_d.append(pltpu.make_async_remote_copy(
                src_ref=ref.at[my_column], dst_ref=ref.at[my_column],
                send_sem=d_send.at[which, step - 1], recv_sem=d_recv.at[which, step - 1],
                device_id={"ctx": target},
            ))
    for copy in sends_d:
        copy.start()
    for copy in sends_d:
        copy.wait_recv()

    for row in range(row_count):
        pieces = []
        for head in range(head_count):
            owner, slot = divmod(row * head_count + head, group_count)
            span = slice(slot * pair_rows, (slot + 1) * pair_rows)
            pieces.append(final[owner % plane, owner // plane, span].astype(jnp.float32))
        for step in range(steps):
            span = slice(step * group_size, (step + 1) * group_size)
            attn_ref[step, row] = jnp.concatenate([p[span] for p in pieces], axis=0).astype(jnp.bfloat16)

    group_of = lax.broadcasted_iota(jnp.int32, (1, LANES), 1) // pair_rows
    masses = []
    for pair in range(pair_count):
        owner, slot = divmod(pair, group_count)
        own_stats = stats[owner % plane, owner // plane]
        all_stats = final_stats[owner % plane, owner // plane]
        factor = jnp.exp(own_stats[0:1] - all_stats[0:1])
        mass = own_stats[1:2] * factor / all_stats[1:2]
        masses.append(jnp.where(group_of == slot, mass, 0.0))
    mass_row = jnp.sum(columns_of(masses), axis=0, keepdims=True)
    for row in range(row_count):
        mass_ref[row] = mass_row[:, row * head_count : (row + 1) * head_count]

    own.wait()
    for copy in sends_a + sends_b + sends_c + sends_d:
        copy.wait_send()
    for turn in turns:
        move(*turn).wait_send()
    for turn in turns:
        move(*turn).wait_recv()


def place_kernel(
    arrived_ref, attn_ref, mass_ref, slot_row, keys_out, values_out, attn_out, mass_out, slot_ref, small_sem, out_sem,
):
    row_count, head_count = keys_out.shape[:2]
    slots = pltpu.make_async_copy(slot_row, slot_ref, small_sem.at[0])
    slots.start()
    small = [
        pltpu.make_async_copy(attn_ref, attn_out, small_sem.at[1]),
        pltpu.make_async_copy(mass_ref, mass_out, small_sem.at[2]),
    ]
    for copy in small:
        copy.start()

    def copies(row, head, slot):
        pair = row * head_count + head
        return [
            pltpu.make_async_copy(arrived_ref.at[slot, which], placed.at[row, head], out_sem.at[2 * pair + which])
            for which, placed in enumerate((keys_out, values_out))
        ]

    slots.wait()
    for row in range(row_count):
        for head in range(head_count):
            for copy in copies(row, head, slot_ref[0, row * head_count + head]):
                copy.start()
    for copy in small:
        copy.wait()
    for row in range(row_count):
        for head in range(head_count):
            for copy in copies(row, head, 0):
                copy.wait()


def local(queries, key_cache, value_cache, row_lengths, kept_tiles, tile_dest):
    device_count = lax.axis_size("ctx")
    plane = 4 if device_count % 4 == 0 and device_count > 4 else 1
    outer = device_count // plane
    row_count, head_count, token_span, width = key_cache.shape
    pair_count = row_count * head_count
    group_count = -(-pair_count // device_count)
    pair_rows = STEPS * (QH // head_count)
    owner_rows = group_count * pair_rows
    slots = device_count * group_count
    assert owner_rows <= LANES and token_span == TILE and tile_dest.shape[2] == device_count
    assert slots <= LANES and pair_count < LANES

    vmem = pl.BlockSpec(memory_space=pltpu.VMEM)
    hbm = pl.BlockSpec(memory_space=pltpu.HBM)
    sems = pltpu.SemaphoreType.DMA
    arrived, attn_out, mass, slot_row = pl.pallas_call(
        functools.partial(main_kernel, device_count, plane, group_count),
        out_shape=(
            pltpu.VMEM((slots, 2, TILE, width), jnp.bfloat16),
            pltpu.VMEM(queries.shape, jnp.bfloat16),
            pltpu.VMEM((row_count, 1, head_count), jnp.float32),
            pltpu.VMEM((1, LANES), jnp.int32),
        ),
        in_specs=[hbm] * 6,
        out_specs=(vmem, vmem, vmem, vmem),
        scratch_shapes=[
            pltpu.SMEM(row_lengths.shape, jnp.int32),
            pltpu.SMEM((row_count, STEPS, kept_tiles.shape[2]), jnp.int32),
            pltpu.VMEM(tile_dest.shape, jnp.int32),
            pltpu.VMEM((1, LANES), jnp.int32),
            pltpu.SMEM((1, LANES), jnp.int32),
            sems((2,)),
            pltpu.VMEM(queries.shape, jnp.bfloat16),
            pltpu.VMEM(key_cache.shape, jnp.bfloat16),
            pltpu.VMEM(value_cache.shape, jnp.bfloat16),
            sems((5,)),
            pltpu.VMEM((slots, 2, TILE, width), jnp.bfloat16),
            pltpu.VMEM((plane, outer, owner_rows, width), jnp.float32),
            pltpu.VMEM((device_count, LANES, LANES), jnp.float32),
            pltpu.VMEM((plane, outer, STAT_ROWS, LANES), jnp.float32),
            pltpu.VMEM((plane - 1, outer, owner_rows, width), jnp.float32),
            pltpu.VMEM((plane - 1, outer, STAT_ROWS, LANES), jnp.float32),
            pltpu.VMEM((outer, owner_rows, width), jnp.float32),
            pltpu.VMEM((outer, STAT_ROWS, LANES), jnp.float32),
            pltpu.VMEM((outer - 1, owner_rows, width), jnp.float32),
            pltpu.VMEM((outer - 1, STAT_ROWS, LANES), jnp.float32),
            pltpu.VMEM((plane, outer, owner_rows, width), jnp.bfloat16),
            pltpu.VMEM((plane, outer, STAT_ROWS, LANES), jnp.float32),
            sems,
            sems((device_count,)),
            sems((device_count,)),
            sems((2, plane - 1)),
            sems((2, plane - 1)),
            sems((2, outer - 1)),
            sems((2, outer - 1)),
            sems((2, outer - 1)),
            sems((2, outer - 1)),
            sems((2, plane - 1)),
            sems((2, plane - 1)),
        ],
        compiler_params=pltpu.CompilerParams(
            collective_id=0, has_side_effects=True, vmem_limit_bytes=32 * 1024 * 1024
        ),
        name="attend_and_move",
    )(*(
        pltpu.with_memory_space_constraint(x, pltpu.HBM)
        for x in (row_lengths, jnp.swapaxes(kept_tiles, 0, 1), tile_dest, queries, key_cache, value_cache)
    ))

    moved_keys, moved_values, attn_out, tile_mass = pl.pallas_call(
        place_kernel,
        out_shape=(
            jax.ShapeDtypeStruct(key_cache.shape, jnp.bfloat16),
            jax.ShapeDtypeStruct(value_cache.shape, jnp.bfloat16),
            jax.ShapeDtypeStruct(attn_out.shape, attn_out.dtype),
            jax.ShapeDtypeStruct(mass.shape, mass.dtype),
        ),
        in_specs=[vmem] * 4,
        out_specs=(hbm,) * 4,
        scratch_shapes=[
            pltpu.SMEM((1, LANES), jnp.int32),
            sems((3,)),
            sems((2 * pair_count,)),
        ],
        compiler_params=pltpu.CompilerParams(vmem_limit_bytes=8 * 1024 * 1024),
        name="place",
    )(arrived, attn_out, mass, slot_row)
    return attn_out, jnp.swapaxes(tile_mass, 1, 2), moved_keys, moved_values


def solution(mesh):
    in_specs = (
        P(None, "grp", None, None),
        P("grp", None, "ctx", None),
        P("grp", None, "ctx", None),
        P("grp"),
        P(None, "grp", None),
        P("grp", None, None),
    )
    out_specs = (
        P(None, "grp", None, None),
        P("grp", None, "ctx"),
        P("grp", None, "ctx", None),
        P("grp", None, "ctx", None),
    )
    return jax.shard_map(local, mesh=mesh, in_specs=in_specs, out_specs=out_specs, check_vma=False)
```
